32 devices in a mesh: depth: 4 (over z), tile: 8 (over y, x, core).
Axes of the slice: x: 2, y: 2, z: 4, core: 2. Of those that a mesh axis runs over, the one named last changes fastest.
Arguments:
- transmission: bfloat16 [2, 8, 2048, 2048], P(None, 'depth', 'tile')
- probe: float32 [2, 128, 128], replicated, may hold values from -6 to 6
- propagator: float32 [128, 128], replicated, may hold values from -3.140625 to 3.140625
- measured: float32 [64, 128, 128], P('tile'), may hold values from 0.2 to 3
- positions: int32 [64, 2], P('tile'), may hold values from 0 to 1920, as said below
- counts: int32 [8], P('tile'), may hold values from 1 to 8, as said below
Outputs:
- object_grad: float32 [2, 8, 2048, 2048], P(None, 'depth', 'tile')
The draws below stay inside these ranges and needn't reach their ends.
Inputs may be any that keep to these rules, and one draw needn't show every extreme that they name: `positions`: A window's first row lies from 0 to 256 in the strip's rows extended by 64 above, its first column from 0 to 1920; both ends of both ranges occur in every draw. `counts`: some strip has all 8 slots live and some strip only one.
All inputs are finite; a program needn't handle non-finite values.
Results may differ from the reference program's by a relative error of at most 0.0003.
Values may be sent and summed in bfloat16 or wider, within the bound.
No kernel may reach another device: no remote copies, remote signals or barrier semaphores. Data moves between devices by JAX's collectives and lax.ppermute only.
A program may use at most 128 MiB of HBM per device.

```python
import math
import jax
import jax.numpy as jnp
from jax import lax

PROBE = 128
W = 2048
TR = 256
CAP = 8
SLICES = 8
TILES = 8
ROWS = 2048


def draw_transmission(key, part):
    first, second = jax.random.split(key)
    shape = (SLICES, ROWS, W)
    real_part = jax.random.uniform(first, shape, jnp.float32, 0.5, 1.0)
    imag_part = jax.random.uniform(second, shape, jnp.float32, -0.5, 0.5)
    return jnp.stack([real_part, imag_part]).astype(jnp.bfloat16)


def draw_positions(key, part):
    keys = jax.random.split(key, 3)
    total = TILES * CAP
    rows_drawn = jax.random.randint(keys[0], (total,), 0, TR + 1)
    cols_drawn = jax.random.randint(keys[1], (total,), 0, W - PROBE + 1)
    marks = jax.random.randint(keys[2], (2,), 0, total)
    rows_drawn = rows_drawn.at[marks[0]].set(TR).at[(marks[0] + 1) % total].set(0)
    cols_drawn = cols_drawn.at[marks[1]].set(W - PROBE).at[(marks[1] + 1) % total].set(0)
    return jnp.stack([rows_drawn, cols_drawn], 1).astype(jnp.int32)


def draw_counts(key, part):
    first, second = jax.random.split(key)
    drawn = jax.random.randint(first, (TILES,), 1, CAP + 1)
    fullest = jax.random.randint(second, (), 0, TILES)
    drawn = drawn.at[fullest].set(CAP).at[(fullest + 1) % TILES].set(1)
    return drawn.astype(jnp.int32)


def block_scale(key, extent, cuts, smallest, largest):
    def one(dim, parts):
        heights = jax.random.uniform(jax.random.fold_in(jax.random.fold_in(key, 6), dim), (parts,), jnp.float32, smallest / len(cuts), largest / len(cuts))
        return jnp.repeat(jnp.exp(heights), extent[dim] // parts).reshape((-1,) + (1,) * (len(extent) - dim - 1))

    loudness = one(*cuts[0])
    for cut in cuts[1:]:
        loudness = loudness * one(*cut)
    return loudness


def normal_values(key, shape, spread, bound, held_as=jnp.bfloat16):
    return jnp.clip(spread * jax.random.normal(key, shape, jnp.float32), -bound, bound).astype(held_as)


def setup_inputs(seed: int = 0) -> dict:
    key_list = jax.random.split(jax.random.key(seed), 7)
    return {
        "transmission": draw_transmission(jax.random.fold_in(key_list[6], 71), 0),
        "probe": normal_values(key_list[1], (2, PROBE, PROBE), 1.0, 6.0, jnp.float32),
        "propagator": jnp.clip(jax.random.uniform(key_list[2], (PROBE, PROBE), jnp.float32, -3.140625, 3.140625), -3.140625, 3.140625),
        "measured": jnp.clip(jnp.exp(math.log(3.0) - 2.7080502 * jax.random.uniform(key_list[3], (TILES * CAP, PROBE, PROBE), jnp.float32) ** block_scale(key_list[3], (TILES * CAP, PROBE, PROBE), ((0, 8),), -0.2, 0.2)), 0.2, 3.0),
        "positions": draw_positions(jax.random.fold_in(key_list[6], 71), 0),
        "counts": draw_counts(jax.random.fold_in(key_list[6], 71), 0),
    }


DELTA = 0.1

def fourier(field):
    return jnp.fft.fft2(field, norm='ortho')

def inverse(field):
    return jnp.fft.ifft2(field, norm='ortho')

def reference(transmission, probe, propagator, measured, positions, counts):
    rows_all = transmission.shape[2]
    halo_rows = PROBE // 2
    objects = transmission.astype(jnp.float32)
    kernel = jnp.cos(propagator) + 1j * jnp.sin(propagator)
    probe_wave = probe[0] + 1j * probe[1]
    zero_index = jnp.zeros((), jnp.int32)

    def one_tile(tile):
        tile = tile.astype(jnp.int32)
        offsets = ((tile * TR - halo_rows + jnp.arange(TR + 2 * halo_rows, dtype=jnp.int32)) % rows_all).astype(jnp.int32)
        strip = jnp.take(objects, offsets, axis=2)
        corners = lax.dynamic_slice_in_dim(positions, (tile * CAP).astype(jnp.int32), CAP, 0).astype(jnp.int32)
        amplitudes = lax.dynamic_slice_in_dim(measured, (tile * CAP).astype(jnp.int32), CAP, 0)
        count = counts[tile]

        def one_position(corner, amplitude, slot):
            starts = (zero_index, zero_index, corner[0].astype(jnp.int32), corner[1].astype(jnp.int32))
            window = lax.dynamic_slice(strip, starts, (2, SLICES, PROBE, PROBE))
            trans = window[0] + 1j * window[1]
            wave = probe_wave
            waves = []
            exit_wave = wave
            for level in range(SLICES):
                waves.append(wave)
                exit_wave = wave * trans[level]
                if level + 1 < SLICES:
                    wave = inverse(kernel * fourier(exit_wave))
            far = fourier(exit_wave)
            modulus = jnp.sqrt(far.real ** 2 + far.imag ** 2 + DELTA)
            live = (slot < count).astype(far.real.dtype)
            grad = inverse(live * (modulus - amplitude) / modulus * far)
            pieces = [None] * SLICES
            for level in reversed(range(SLICES)):
                pieces[level] = jnp.conj(waves[level]) * grad
                if level > 0:
                    back = jnp.conj(trans[level]) * grad
                    grad = inverse(jnp.conj(kernel) * fourier(back))
            stacked = jnp.stack(pieces)
            return jnp.stack([stacked.real, stacked.imag])
        grads = jax.vmap(one_position)(corners, amplitudes, jnp.arange(CAP, dtype=jnp.int32))

        def add_window(index, total):
            corner = corners[index]
            starts = (zero_index, zero_index, corner[0].astype(jnp.int32), corner[1].astype(jnp.int32))
            current = lax.dynamic_slice(total, starts, (2, SLICES, PROBE, PROBE))
            return lax.dynamic_update_slice(total, current + grads[index], starts)
        total = jnp.zeros((2, SLICES, TR + 2 * halo_rows, W), grads.dtype)
        return lax.fori_loop(0, CAP, add_window, total)
    strips = lax.map(one_tile, jnp.arange(TILES, dtype=jnp.int32))
    center = strips[:, :, :, halo_rows:halo_rows + TR]
    upper = jnp.roll(strips[:, :, :, :halo_rows], -1, axis=0)
    lower = jnp.roll(strips[:, :, :, TR + halo_rows:], 1, axis=0)
    center = center.at[:, :, :, :halo_rows].add(lower)
    center = center.at[:, :, :, TR - halo_rows:].add(upper)
    return jnp.transpose(center, (1, 2, 0, 3, 4)).reshape(2, SLICES, rows_all, W).astype(jnp.float32)
```

```python
import functools
import math

import jax
import jax.numpy as jnp
import numpy as np
from jax import lax
from jax.experimental import pallas as pl
from jax.experimental.pallas import tpu as pltpu
from jax.sharding import PartitionSpec as P

DELTA = 0.1
F32, BF16, I32, I16 = jnp.float32, jnp.bfloat16, jnp.int32, jnp.int16
LANES = 128
PACK = 16
STEPS = 32767.0
VMEM = pl.BlockSpec(memory_space=pltpu.VMEM)
SMEM = pl.BlockSpec(memory_space=pltpu.SMEM)
ANY = pl.BlockSpec(memory_space=pl.ANY)


def shifted(array, axis, by):
    count = lax.axis_size(axis)
    return lax.ppermute(array, axis, [(i, (i + by) % count) for i in range(count)])


def matmul(a, b):
    return jnp.dot(a, b, preferred_element_type=F32)


def one_hot(shape, difference):
    rows = lax.broadcasted_iota(I32, shape, 0)
    columns = lax.broadcasted_iota(I32, shape, 1)
    return jnp.where(columns - rows == difference, 1.0, 0.0).astype(BF16)


def column_block(column, columns, width):
    start = jnp.minimum(column // LANES * LANES, columns - width - LANES)
    return pl.multiple_of(start, LANES), column - start


def dft_tables(width):
    index = np.arange(width)
    angle = (index[:, None] * index[None, :] % width) * (2.0 * math.pi / width)
    scale = 1.0 / math.sqrt(width)
    parts = []
    for table in (np.cos(angle) * scale, np.sin(angle) * scale):
        high = table.astype(jnp.bfloat16)
        parts += [high, (table - high.astype(np.float64)).astype(jnp.bfloat16)]
    return np.stack(parts)


def own_kernel(depth, pos, me, source, *refs):
    cleans, others = refs[:depth], refs[depth : 2 * depth]
    held, columns_at, rows_at, sems = refs[2 * depth :]
    per, levels, _, half, width = cleans[0].shape
    tile_rows, columns = source.shape[2:]
    region = width + PACK
    copies = []
    for comp in range(2):
        for level in range(levels):
            copy = pltpu.make_async_copy(
                source.at[comp, level], held.at[comp, level], sems.at[comp, level]
            )
            copy.start()
            copies.append(copy)

    def corner(slot):
        row, column = pos[slot, 0], pos[slot, 1]
        first = jnp.clip((row - half + tile_rows) // PACK * PACK - tile_rows, 0, tile_rows - region)
        return row, pl.multiple_of(first, PACK), column

    for slot in range(depth * per):
        row, first, column = corner(slot)
        _, place = column_block(column, columns, width)
        columns_at[slot] = one_hot((width + LANES, width), -place)
        lead = jnp.where(row >= half, 0, half)
        index = lax.broadcasted_iota(I32, (width, region), 0)
        target = index + jnp.where(index < half, lead, -lead) + row - half - first
        hit = lax.broadcasted_iota(I32, (width, region), 1) == target
        rows_at[slot] = jnp.where(hit, 1.0, 0.0).astype(BF16)
    for comp in range(2):
        for level in range(levels):
            copies[comp * levels + level].wait()
            for by in range(depth):
                for b in range(per):
                    slot = lax.rem(me[0] + by, depth) * per + b
                    row, first, column = corner(slot)
                    start, _ = column_block(column, columns, width)
                    block = held[comp, level, pl.ds(first, region), pl.ds(start, width + LANES)]
                    picked = matmul(block, columns_at[slot]).astype(BF16)
                    picked = matmul(rows_at[slot], picked).astype(BF16)
                    cleans[by][b, level, comp] = picked[:half]
                    others[by][b, level, comp] = picked[half:]


def own_windows(pos, me, transmission, depth, width):
    levels, tile_rows, columns = transmission.shape[1:]
    slots = pos.shape[0]
    per = slots // depth
    piece = jax.ShapeDtypeStruct((per, levels, 2, width // 2, width), BF16)
    return pl.pallas_call(
        functools.partial(own_kernel, depth),
        name="own_windows",
        out_shape=[piece] * (2 * depth),
        in_specs=[SMEM, SMEM, ANY],
        out_specs=[VMEM] * (2 * depth),
        scratch_shapes=[
            pltpu.VMEM(transmission.shape, BF16),
            pltpu.VMEM((slots, width + LANES, width), BF16),
            pltpu.VMEM((slots, width, width + PACK), BF16),
            pltpu.SemaphoreType.DMA((2, levels)),
        ],
    )(pos, me, transmission)


def rim_kernel(pos_prev, pos_next, source, to_prev, to_next, low, high, sems):
    slots, levels, _, half, width = to_prev.shape
    tile_rows, columns = source.shape[2:]
    first = pltpu.make_async_copy(source.at[:, :, pl.ds(0, half), :], low, sems.at[0])
    second = pltpu.make_async_copy(
        source.at[:, :, pl.ds(tile_rows - half, half), :], high, sems.at[1]
    )
    first.start()
    second.start()
    first.wait()
    second.wait()

    def pieces(edge, row, column, out, offset, needed):
        @pl.when(needed)
        def _():
            start, place = column_block(column, columns, width)
            at_columns = one_hot((width + LANES, width), -place)
            at_rows = one_hot((half, half), offset)
            for comp in range(2):
                for level in range(levels):
                    block = edge[comp, level, :, pl.ds(start, width + LANES)]
                    picked = matmul(block, at_columns).astype(BF16)
                    out[level, comp] = matmul(at_rows, picked).astype(BF16)

        @pl.when(jnp.logical_not(needed))
        def _():
            out[...] = jnp.zeros_like(out)

    for slot in range(slots):
        row, column = pos_next[slot, 0], pos_next[slot, 1]
        pieces(high, row, column, to_next.at[slot], row, row < half)
        row, column = pos_prev[slot, 0], pos_prev[slot, 1]
        pieces(low, row, column, to_prev.at[slot], row - tile_rows, row > tile_rows - half)


def rim_pieces(pos_prev, pos_next, transmission, width):
    levels, tile_rows, columns = transmission.shape[1:]
    slots = pos_prev.shape[0]
    piece = jax.ShapeDtypeStruct((slots, levels, 2, width // 2, width), BF16)
    edge = pltpu.VMEM((2, levels, width // 2, columns), BF16)
    return pl.pallas_call(
        rim_kernel,
        name="rim_pieces",
        out_shape=[piece, piece],
        in_specs=[SMEM, SMEM, ANY],
        out_specs=[VMEM, VMEM],
        scratch_shapes=[edge, edge, pltpu.SemaphoreType.DMA((2,))],
    )(pos_prev, pos_next, transmission)


def merge_kernel(depth, pos, me, from_prev, from_next, *refs):
    others, mixed = refs[:depth], refs[depth:]
    per, half = others[0].shape[0], others[0].shape[3]
    for by in range(depth):
        for b in range(per):
            slot = lax.rem(me[0] + by, depth) * per + b
            upper = pos[slot, 0] < half

            @pl.when(upper)
            def _():
                mixed[by][b] = others[by][b] + from_prev[slot]

            @pl.when(jnp.logical_not(upper))
            def _():
                mixed[by][b] = others[by][b] + from_next[slot]


def merged(pos, me, from_prev, from_next, others):
    depth = len(others)
    return pl.pallas_call(
        functools.partial(merge_kernel, depth),
        name="merged",
        out_shape=[jax.ShapeDtypeStruct(o.shape, o.dtype) for o in others],
        in_specs=[SMEM, SMEM] + [VMEM] * (2 + depth),
        out_specs=[VMEM] * depth,
    )(pos, me, from_prev, from_next, *others)


def split(value):
    high = value.astype(BF16)
    return high, (value - high.astype(F32)).astype(BF16)


def build_tables(tables, right, left):
    cos_high, cos_low, sin_high, sin_low = (tables[i] for i in range(4))

    def pair(cos, sin):
        minus = (-sin.astype(F32)).astype(BF16)
        forward = jnp.concatenate(
            [jnp.concatenate([cos, minus], 1), jnp.concatenate([sin, cos], 1)], 0
        )
        inverse = jnp.concatenate(
            [jnp.concatenate([cos, sin], 1), jnp.concatenate([minus, cos], 1)], 0
        )
        return forward, inverse

    one_high, two_high = pair(cos_high, sin_high)
    one_low, two_low = pair(cos_low, sin_low)
    right[0] = jnp.concatenate([one_high, one_high, one_low], 0)
    right[1] = jnp.concatenate([two_high, two_high, two_low], 0)
    left[0] = jnp.concatenate([two_high, two_high, two_low], 1)
    left[1] = jnp.concatenate([one_high, one_high, one_low], 1)


def along_columns(wave, table):
    width = wave[0].shape[0]
    high, low = split(jnp.concatenate(wave, 1))
    out = matmul(jnp.concatenate([high, low, high], 1), table)
    return out[:, :width], out[:, width:]


def along_rows(wave, table):
    width = wave[0].shape[0]
    high, low = split(jnp.concatenate(wave, 0))
    out = matmul(table, jnp.concatenate([high, low, high], 0))
    return out[:width], out[width:]


def times(a, b):
    return a[0] * b[0] - a[1] * b[1], a[0] * b[1] + a[1] * b[0]


def conj_times(a, b):
    return a[0] * b[0] + a[1] * b[1], a[0] * b[1] - a[1] * b[0]


def waves_kernel(depth, pos, me, counts, *refs):
    cleans, mixed = refs[:depth], refs[depth : 2 * depth]
    probe, filt, measured, tables = refs[2 * depth : 2 * depth + 4]
    codes = refs[2 * depth + 4 : 3 * depth + 4]
    window, waves, grads, right, left = refs[3 * depth + 4 :]
    per, levels, _, half, width = cleans[0].shape
    slices = depth * levels
    last = slices - 1
    every = range(per)
    build_tables(tables, right, left)
    for by in range(depth):
        origin = lax.rem(me[0] + depth - by, depth)
        for b in every:
            row = pos[me[0] * per + b, 0]
            lead = pl.multiple_of(jnp.where(row >= half, 0, half), half)
            rest = pl.multiple_of(half - lead, half)
            for level in range(levels):
                for comp in range(2):
                    at = window.at[b, origin * levels + level, comp]
                    at[pl.ds(lead, half), :] = cleans[by][b, level, comp]
                    at[pl.ds(rest, half), :] = mixed[by][b, level, comp]

    def trans(b, s):
        return window[b, s, 0].astype(F32), window[b, s, 1].astype(F32)

    def load(b, s):
        return waves[s, b, 0], waves[s, b, 1]

    def store(b, s, wave):
        waves[s, b, 0] = wave[0]
        waves[s, b, 1] = wave[1]

    def fourier(group):
        group = [along_columns(v, right[0]) for v in group]
        return [along_rows(v, left[0]) for v in group]

    def inverse(group):
        group = [along_rows(v, left[1]) for v in group]
        return [along_columns(v, right[1]) for v in group]

    for b in every:
        store(b, 0, (probe[0], probe[1]))

    def forward(s, carry):
        group = fourier([times(load(b, s), trans(b, s)) for b in every])
        group = inverse([times(v, (filt[0], filt[1])) for v in group])
        for b in every:
            store(b, s + 1, group[b])
        return carry

    lax.fori_loop(0, last, forward, 0)
    far = fourier([times(load(b, last), trans(b, last)) for b in every])
    group = []
    for b in every:
        modulus = jnp.sqrt(far[b][0] * far[b][0] + far[b][1] * far[b][1] + DELTA)
        live = jnp.where(me[0] * per + b < counts[0], 1.0, 0.0).astype(F32)
        weight = live * (modulus - measured[b]) / modulus
        group.append((weight * far[b][0], weight * far[b][1]))
    group = inverse(group)
    for b in every:
        store(b, slices, group[b])

    def emit(b, s, grad):
        piece = conj_times(load(b, s), grad)
        grads[s, b, 0] = piece[0]
        grads[s, b, 1] = piece[1]

    def backward(step, carry):
        s = last - step
        group = [load(b, slices) for b in every]
        for b in every:
            emit(b, s, group[b])
        group = fourier([conj_times(trans(b, s), group[b]) for b in every])
        group = inverse([conj_times((filt[0], filt[1]), v) for v in group])
        for b in every:
            store(b, slices, group[b])
        return carry

    lax.fori_loop(0, last, backward, 0)
    for b in every:
        emit(b, 0, load(b, slices))

    planes = per * levels * 2
    for by in range(depth):
        target = lax.rem(me[0] + by, depth)
        exponents = []
        for b in every:
            for level in range(levels):
                for comp in range(2):
                    value = grads[target * levels + level, b, comp]
                    biggest = jnp.max(jnp.abs(value), axis=0, keepdims=True)
                    power = jnp.floor(jnp.log2(jnp.maximum(biggest, 1e-30))) + 1.0
                    scaled = value * (jnp.exp2(-power) * STEPS)
                    code = jnp.clip(jnp.round(scaled), -STEPS, STEPS)
                    code = code.astype(I32).astype(I16)
                    plane = (b * levels + level) * 2 + comp
                    codes[by][pl.ds(plane * half, half), :] = code[:half]
                    codes[by][pl.ds((planes + plane) * half + planes, half), :] = code[half:]
                    exponents.append(power)
        exponents = jnp.concatenate(exponents, 0).astype(I32).astype(I16)
        codes[by][pl.ds(planes * half, planes), :] = exponents


def window_grads(pos, me, counts, cleans, mixed, probe, filt, measured, tables):
    depth = len(cleans)
    per, levels, _, half, width = cleans[0].shape
    slices = depth * levels
    planes = per * levels * 2
    message = jax.ShapeDtypeStruct((planes * (width + 1), width), I16)
    return pl.pallas_call(
        functools.partial(waves_kernel, depth),
        name="window_grads",
        out_shape=[message] * depth,
        in_specs=[SMEM] * 3 + [VMEM] * (2 * depth + 4),
        out_specs=[VMEM] * depth,
        scratch_shapes=[
            pltpu.VMEM((per, slices, 2, width, width), BF16),
            pltpu.VMEM((slices + 1, per, 2, width, width), F32),
            pltpu.VMEM((slices, per, 2, width, width), F32),
            pltpu.VMEM((2, 6 * width, 2 * width), BF16),
            pltpu.VMEM((2, 2 * width, 6 * width), BF16),
        ],
    )(pos, me, counts, *cleans, *mixed, probe, filt, measured, tables)


def decoded(code, power):
    return code.astype(I32).astype(F32) * (jnp.exp2(power.astype(I32).astype(F32)) * (1.0 / STEPS))


def add_at(total, row, column, value):
    block, place = column // LANES, lax.rem(column, LANES)
    height = value.shape[0]
    value = pltpu.roll(value, place, 1)
    here = lax.broadcasted_iota(I32, value.shape, 1) >= place
    at = total.at[block, pl.ds(row, height), :]
    at[...] += jnp.where(here, value, 0.0)
    at = total.at[block + 1, pl.ds(row, height), :]
    at[...] += jnp.where(here, 0.0, value)


def inner_kernel(depth, levels, pos, me, *refs):
    codes = refs[:depth]
    out, rims, total, sems = refs[depth:]
    width = codes[0].shape[1]
    planes = codes[0].shape[0] // (width + 1)
    half = width // 2
    per = planes // (2 * levels)
    tile_rows = out.shape[2]
    blocks = rims.shape[3]
    copies = []
    for comp in range(2):
        for level in range(levels):
            at = total.at[comp, level]
            at[...] = jnp.zeros(at.shape, F32)
            for by in range(depth):
                for b in range(per):
                    slot = lax.rem(me[0] + depth - by, depth) * per + b
                    plane = (b * levels + level) * 2 + comp
                    power = codes[by][pl.ds(planes * half, planes), :][plane : plane + 1]
                    upper = decoded(codes[by][pl.ds(plane * half, half), :], power)
                    lower = decoded(
                        codes[by][pl.ds((planes + plane) * half + planes, half), :], power
                    )
                    value = jnp.concatenate([upper, lower], 0)
                    add_at(at, pos[slot, 0], pos[slot, 1], value)
            for block in range(blocks):
                copy = pltpu.make_async_copy(
                    at.at[block, pl.ds(width, tile_rows - width), :],
                    out.at[
                        comp, level, pl.ds(half, tile_rows - width), pl.ds(block * LANES, LANES)
                    ],
                    sems.at[comp, level, block],
                )
                copy.start()
                copies.append(copy)
                rims[comp, level, 0, block] = at[block, pl.ds(half, half), :]
                rims[comp, level, 1, block] = at[block, pl.ds(tile_rows, half), :]
    for copy in copies:
        copy.wait()


def inner_sum(pos, me, codes, levels, tile_rows, columns):
    depth = len(codes)
    width = codes[0].shape[1]
    half = width // 2
    blocks = columns // LANES
    return pl.pallas_call(
        functools.partial(inner_kernel, depth, levels),
        name="inner_sum",
        out_shape=[
            jax.ShapeDtypeStruct((2, levels, tile_rows, columns), F32),
            jax.ShapeDtypeStruct((2, levels, 2, blocks, half, LANES), F32),
        ],
        in_specs=[SMEM, SMEM] + [VMEM] * depth,
        out_specs=[ANY, VMEM],
        scratch_shapes=[
            pltpu.VMEM((2, levels, blocks + 1, tile_rows + width, LANES), F32),
            pltpu.SemaphoreType.DMA((2, levels, blocks)),
        ],
    )(pos, me, *codes)


def outer_kernel(depth, pos_prev, pos_next, me, from_prev, from_next, rims, part, out, total, sems):
    _, levels, _, blocks, half, _ = rims.shape
    tile_rows = out.shape[2]
    planes = from_prev.shape[0] // depth // (half + 1)
    per = planes // (2 * levels)
    step = planes * (half + 1)
    copies = []
    for comp in range(2):
        for level in range(levels):
            for side in range(2):
                at = total.at[comp, level, side]
                at[pl.ds(0, blocks), pl.ds(half, half), :] = rims[comp, level, side]
            for by in range(depth):
                for b in range(per):
                    slot = lax.rem(me[0] + depth - by, depth) * per + b
                    plane = (b * levels + level) * 2 + comp
                    row, column = pos_prev[slot, 0], pos_prev[slot, 1]

                    @pl.when(row > tile_rows - half)
                    def _():
                        power = from_prev[pl.ds(by * step, planes), :][plane : plane + 1]
                        code = from_prev[pl.ds(by * step + planes + plane * half, half), :]
                        at = total.at[comp, level, 0]
                        add_at(at, row - tile_rows + half, column, decoded(code, power))

                    row_next, column_next = pos_next[slot, 0], pos_next[slot, 1]

                    @pl.when(row_next < half)
                    def _():
                        power = from_next[pl.ds(by * step + planes * half, planes), :]
                        code = from_next[pl.ds(by * step + plane * half, half), :]
                        at = total.at[comp, level, 1]
                        value = decoded(code, power[plane : plane + 1])
                        add_at(at, row_next + half, column_next, value)

            for side in range(2):
                for block in range(blocks):
                    copy = pltpu.make_async_copy(
                        total.at[comp, level, side, block, pl.ds(half, half), :],
                        out.at[
                            comp,
                            level,
                            pl.ds(side * (tile_rows - half), half),
                            pl.ds(block * LANES, LANES),
                        ],
                        sems.at[comp, level, side, block],
                    )
                    copy.start()
                    copies.append(copy)
    for copy in copies:
        copy.wait()


def outer_sum(pos_prev, pos_next, me, from_prev, from_next, rims, part, depth):
    _, levels, _, blocks, half, _ = rims.shape
    return pl.pallas_call(
        functools.partial(outer_kernel, depth),
        name="outer_sum",
        out_shape=jax.ShapeDtypeStruct(part.shape, F32),
        in_specs=[SMEM] * 3 + [VMEM] * 3 + [ANY],
        out_specs=ANY,
        scratch_shapes=[
            pltpu.VMEM((2, levels, 2, blocks + 1, 3 * half, LANES), F32),
            pltpu.SemaphoreType.DMA((2, levels, 2, blocks)),
        ],
        input_output_aliases={6: 0},
    )(pos_prev, pos_next, me, from_prev, from_next, rims, part)


def body(transmission, probe, propagator, measured, positions, counts):
    width = probe.shape[1]
    half = width // 2
    levels, tile_rows, columns = transmission.shape[1:]
    slots = positions.shape[0]
    depth = lax.axis_size("depth")
    per = slots // depth
    me = lax.axis_index("depth").astype(I32)
    me_ref = me.reshape(1)
    tables = jnp.asarray(dft_tables(width))
    pos_prev = shifted(positions, "tile", 1)
    pos_next = shifted(positions, "tile", -1)
    pieces = own_windows(positions, me_ref, transmission, depth, width)
    cleans, others = pieces[:depth], pieces[depth:]
    cleans = [cleans[0]] + [shifted(cleans[by], "depth", by) for by in range(1, depth)]
    to_prev, to_next = rim_pieces(pos_prev, pos_next, transmission, width)
    from_next = shifted(to_prev, "tile", -1)
    from_prev = shifted(to_next, "tile", 1)
    mixed = merged(positions, me_ref, from_prev, from_next, others)
    mixed = [mixed[0]] + [shifted(mixed[by], "depth", by) for by in range(1, depth)]
    filt = jnp.stack([jnp.cos(propagator), jnp.sin(propagator)])
    mine = lax.dynamic_slice_in_dim(measured, me * per, per, 0)
    codes = window_grads(positions, me_ref, counts, cleans, mixed, probe, filt, mine, tables)
    codes = [codes[0]] + [shifted(codes[by], "depth", by) for by in range(1, depth)]
    planes = per * levels * 2
    upper = jnp.concatenate([c[: planes * (half + 1)] for c in codes], 0)
    lower = jnp.concatenate([c[planes * half :] for c in codes], 0)
    from_next = shifted(upper, "tile", -1)
    from_prev = shifted(lower, "tile", 1)
    part, rims = inner_sum(positions, me_ref, codes, levels, tile_rows, columns)
    return outer_sum(pos_prev, pos_next, me_ref, from_prev, from_next, rims, part, depth)


def solution(mesh):
    in_specs = (
        P(None, "depth", "tile", None),
        P(),
        P(),
        P("tile", None, None),
        P("tile", None),
        P("tile"),
    )
    out_specs = P(None, "depth", "tile", None)
    return jax.shard_map(body, mesh=mesh, in_specs=in_specs, out_specs=out_specs, check_vma=False)
```
